32 devices in a mesh: section: 2 (over y), hid: 4 (over x, core), wid: 4 (over z).
Axes of the slice: x: 2, y: 2, z: 4, core: 2. Of those that a mesh axis runs over, the one named last changes fastest.
Arguments:
- w_first: bfloat16 [2, 5120, 20480], P('section', 'wid', 'hid'), may hold values from -0.078125 to 0.078125
- w_second: bfloat16 [2, 20480, 5120], P('section', 'hid', 'wid'), may hold values from -0.0390625 to 0.0390625
- saved_inputs: bfloat16 [2, 2, 256, 5120], P('section', None, None, 'wid'), may hold values from -0.75 to 0.75
- saved_hidden: bfloat16 [2, 2, 256, 20480], P('section', None, None, 'hid'), may hold values from -0.375 to 0.375
- cotangent: bfloat16 [2, 256, 5120], P(None, None, 'wid'), may hold values from -6 to 6
Outputs:
- grad_first: float32 [2, 5120, 20480], P('section', 'wid', 'hid')
- grad_second: float32 [2, 20480, 5120], P('section', 'hid', 'wid')
- input_grads: bfloat16 [2, 2, 256, 5120], P('section', None, 'hid', 'wid')
The draws below stay inside these ranges and needn't reach their ends.
All inputs are finite; a program needn't handle non-finite values.
Results may differ from the reference program's by a relative error of at most 0.0055.
Values may be sent and summed in bfloat16 or wider, within the bound.
No kernel may reach another device: no remote copies, remote signals or barrier semaphores. Data moves between devices by JAX's collectives and lax.ppermute only.
A program may use at most 192 MiB of HBM per device.

```python
import jax
import jax.numpy as jnp

D = 5120
FF = 20480
ROWS = 256
MICRO = 2
SECTIONS = 2


def block_scale(key, extent, split, low, high):
    level = 1.0
    for dim, shards_of in split:
        steps = jax.random.uniform(jax.random.fold_in(jax.random.fold_in(key, 6), dim), (shards_of,), jnp.float32, low / len(split), high / len(split))
        level = level * jnp.repeat(jnp.exp(steps), extent[dim] // shards_of).reshape((-1,) + (1,) * (len(extent) - 1 - dim))
    return level


def bell_draw(own_key, shape, deviation, most, split=(), held_as=jnp.bfloat16):
    values = deviation * jax.random.normal(own_key, shape, jnp.float32)
    if split:
        values = values * block_scale(own_key, shape, split, -0.22, 0.18)
    return jnp.clip(values, -most, most).astype(held_as)


def setup_inputs(seed: int = 0) -> dict:
    seeds = jax.random.split(jax.random.key(seed), 6)
    w_first = bell_draw(seeds[0], (SECTIONS, D, FF), D ** -0.5, 0.078125, ((0, 2), (1, 4), (2, 4)))
    w_second = bell_draw(seeds[1], (SECTIONS, FF, D), FF ** -0.5, 0.0390625, ((0, 2), (1, 4), (2, 4)))
    saved_inputs = bell_draw(seeds[2], (SECTIONS, MICRO, ROWS, D), 0.125, 0.75, ((0, 2), (3, 4)))
    saved_hidden = bell_draw(seeds[3], (SECTIONS, MICRO, ROWS, FF), 0.0625, 0.375, ((0, 2), (3, 4)))
    cotangent = bell_draw(seeds[4], (MICRO, ROWS, D), 1.0, 6.0, ((2, 4),))
    return dict(w_first=w_first, w_second=w_second, saved_inputs=saved_inputs, saved_hidden=saved_hidden, cotangent=cotangent)


def layer_grads(inputs, pre_act, incoming, weight_first, weight_second):
    activated = jnp.maximum(pre_act, 0)
    summed = jnp.dot(incoming, weight_second.T, preferred_element_type=jnp.float32)
    hidden_grad = jnp.where(pre_act > 0, summed, jnp.float32(0.0)).astype(jnp.bfloat16)
    second = jnp.dot(activated.T, incoming, preferred_element_type=jnp.float32)
    first = jnp.dot(inputs.T, hidden_grad, preferred_element_type=jnp.float32)
    input_grad = jnp.dot(hidden_grad, weight_first.T, preferred_element_type=jnp.float32).astype(jnp.bfloat16)
    return first, second, input_grad


def reference(w_first, w_second, saved_inputs, saved_hidden, cotangent):
    first_sums = [jnp.zeros((D, FF), jnp.float32), jnp.zeros((D, FF), jnp.float32)]
    second_sums = [jnp.zeros((FF, D), jnp.float32), jnp.zeros((FF, D), jnp.float32)]
    results = [[None] * MICRO, [None] * MICRO]
    for micro_index in range(MICRO):
        incoming = cotangent[micro_index]
        for section_index in (1, 0):
            first, second, incoming = layer_grads(saved_inputs[section_index, micro_index], saved_hidden[section_index, micro_index], incoming, w_first[section_index], w_second[section_index])
            first_sums[section_index] = first_sums[section_index] + first
            second_sums[section_index] = second_sums[section_index] + second
            results[section_index][micro_index] = incoming
    grad_first = jnp.stack(first_sums)
    grad_second = jnp.stack(second_sums)
    input_grads = jnp.stack([jnp.stack(results[0]), jnp.stack(results[1])])
    return grad_first, grad_second, input_grads
```

```python
import functools

import jax
import jax.numpy as jnp
from jax import lax
from jax.experimental import pallas as pl
from jax.experimental.pallas import tpu as pltpu
from jax.sharding import PartitionSpec as P

SUB_CHUNKS = 2
LAG = 2


def exchange(blocks, axis):
    count = lax.axis_size(axis)
    arrived = []
    for shift in range(1, count):
        pairs = [(i, (i + shift) % count) for i in range(count)]
        arrived.append(lax.ppermute(blocks[shift - 1], axis, pairs))
    return arrived


def hand_down(share):
    sections, hids = lax.axis_size("section"), lax.axis_size("hid")
    arrived = []
    for shift in range(hids):
        pairs = [
            (s * hids + h, (s - 1) * hids + (h + shift) % hids)
            for s in range(1, sections)
            for h in range(hids)
        ]
        arrived.append(lax.ppermute(share, ("section", "hid"), pairs))
    return arrived


def estimate(flops, moved):
    return pl.CostEstimate(flops=flops, bytes_accessed=moved, transcendentals=0)


def dot(left, right, left_dim, right_dim):
    return lax.dot_general(
        left, right, (((left_dim,), (right_dim,)), ((), ())), preferred_element_type=jnp.float32
    )


def piece_of(size, wanted):
    fits = [p for p in range(128, wanted + 1, 128) if size % p == 0]
    return fits[-1] if fits else size


def project_kernel(count, hids, place_ref, given_ref, *refs):
    received_refs, refs = refs[:hids], refs[hids:]
    weight_ref, refs = refs[0], refs[1:]
    sent_refs, (own_ref, incoming_ref, turned_ref) = refs[: count - 1], refs[count - 1 :]
    step = pl.program_id(0)
    rows, width = incoming_ref.shape
    sub = rows // hids

    @pl.when((step == 0) & (pl.program_id(1) == 0))
    def _():
        @pl.when(place_ref[0] == 1)
        def _():
            incoming_ref[...] = given_ref[...].reshape(rows, width)

        @pl.when(place_ref[0] != 1)
        def _():
            for k in range(hids):
                start = pl.multiple_of(place_ref[3 + k] * sub, sub)
                incoming_ref[pl.ds(start, sub), :] = received_refs[k][...]

        turned_ref[...] = incoming_ref[...].T

    block = dot(weight_ref[...], turned_ref[...], 1, 0)
    for k in range(count - 1):

        @pl.when(step == k)
        def _(k=k):
            sent_refs[k][...] = block.astype(sent_refs[k].dtype)

    @pl.when(step == count - 1)
    def _():
        own_ref[...] = block


def project(place, given_parts, received, weight, count):
    hidden, width = weight.shape
    hids, _, sub = given_parts.shape[1:4]
    rows = hids * sub
    columns = hidden // count
    piece = piece_of(columns, 1280)
    pieces = columns // piece

    def block_at(own_step):
        def index(k, c, s):
            return (jnp.where(k == own_step, c, jnp.where(k < own_step, 0, pieces - 1)), 0)

        return pl.BlockSpec((piece, rows), index)

    grid_spec = pltpu.PrefetchScalarGridSpec(
        num_scalar_prefetch=1,
        grid=(count, pieces),
        in_specs=[
            pl.BlockSpec((1, hids, 1, sub, width), lambda k, c, s: (s[1], 0, s[2], 0, 0)),
            *[pl.BlockSpec((sub, width), lambda k, c, s: (0, 0)) for _ in range(hids)],
            pl.BlockSpec((piece, width), lambda k, c, s: (s[3 + hids + k] * pieces + c, 0)),
        ],
        out_specs=[
            *[block_at(k) for k in range(count)],
            pl.BlockSpec((rows, width), lambda k, c, s: (0, 0)),
        ],
        scratch_shapes=[pltpu.VMEM((width, rows), jnp.bfloat16)],
    )
    out = pl.pallas_call(
        functools.partial(project_kernel, count, hids),
        grid_spec=grid_spec,
        out_shape=[
            *[jax.ShapeDtypeStruct((columns, rows), jnp.bfloat16) for _ in range(count - 1)],
            jax.ShapeDtypeStruct((columns, rows), jnp.float32),
            jax.ShapeDtypeStruct((rows, width), jnp.bfloat16),
        ],
        cost_estimate=estimate(2 * rows * width * hidden, 2 * width * hidden),
        name="project",
    )(place, given_parts, *received, weight)
    return out[: count - 1], out[count - 1], out[count]


def join_kernel(place_ref, own_ref, *refs):
    arrived_refs, (hidden_ref, out_ref) = refs[:-2], refs[-2:]
    total = own_ref[...]
    for ref in arrived_refs:
        total += ref[...].astype(jnp.float32)
    out_ref[...] = jnp.where(hidden_ref[...] > 0, total, jnp.float32(0.0)).astype(out_ref.dtype)


def join(place, own, arrived, hidden_t):
    columns, rows = own.shape
    piece = piece_of(columns, 640)
    pieces = columns // piece
    here = pl.BlockSpec((piece, rows), lambda n, s: (n, 0))
    grid_spec = pltpu.PrefetchScalarGridSpec(
        num_scalar_prefetch=1,
        grid=(pieces,),
        in_specs=[here]
        + [here for _ in arrived]
        + [pl.BlockSpec((piece, rows), lambda n, s: (s[0] * pieces + n, s[1]))],
        out_specs=here,
    )
    return pl.pallas_call(
        join_kernel,
        grid_spec=grid_spec,
        out_shape=jax.ShapeDtypeStruct(own.shape, jnp.bfloat16),
        cost_estimate=estimate(5 * own.size, 14 * own.size),
        name="join",
    )(place, own, *arrived, hidden_t)


def total_kernel(own_ref, *refs):
    total = own_ref[...]
    for ref in refs[:-1]:
        total += ref[...]
    refs[-1][...] = total.astype(refs[-1].dtype)


def rounded_total(own, arrived):
    return pl.pallas_call(
        total_kernel,
        out_shape=jax.ShapeDtypeStruct(own.shape, jnp.bfloat16),
        cost_estimate=estimate(4 * own.size, 18 * own.size),
        name="total",
    )(own, *arrived)


def back_kernel(hids, place_ref, grads_ref, weight_ref, *refs):
    out_refs, piece_ref = refs[:hids], refs[hids]
    sub = out_refs[0].shape[0]
    piece_ref[...] = dot(weight_ref[...], grads_ref[...], 1, 0).T
    for k in range(hids):
        start = pl.multiple_of(place_ref[k] * sub, sub)
        out_refs[k][...] = piece_ref[pl.ds(start, sub), :]


def back(place, grads, weight, hids):
    hidden, rows = grads.shape
    width = weight.shape[0]
    sub = rows // hids
    piece = piece_of(width, 256)
    grid_spec = pltpu.PrefetchScalarGridSpec(
        num_scalar_prefetch=1,
        grid=(width // piece,),
        in_specs=[
            pl.BlockSpec((hidden, rows), lambda n, s: (0, 0)),
            pl.BlockSpec((piece, hidden), lambda n, s: (n, 0)),
        ],
        out_specs=[pl.BlockSpec((sub, piece), lambda n, s: (0, n)) for _ in range(hids)],
        scratch_shapes=[pltpu.VMEM((rows, piece), jnp.float32)],
    )
    return pl.pallas_call(
        functools.partial(back_kernel, hids),
        grid_spec=grid_spec,
        out_shape=[jax.ShapeDtypeStruct((sub, width), jnp.float32) for _ in range(hids)],
        cost_estimate=estimate(2 * rows * width * hidden, 2 * width * hidden),
        name="back",
    )(place, grads, weight)


def first_kernel(inputs_ref, grads_ref, out_ref):
    grads = jnp.concatenate([grads_ref[c] for c in range(grads_ref.shape[0])], axis=1)
    out_ref[...] = dot(inputs_ref[...], grads, 1, 1)


def first_gradient(inputs_t, slots, chunks):
    width, rows = inputs_t.shape
    _, hidden, chunk_rows = slots.shape
    piece = piece_of(hidden, 640)
    return pl.pallas_call(
        first_kernel,
        grid=(hidden // piece,),
        in_specs=[
            pl.BlockSpec((width, rows), lambda n: (0, 0)),
            pl.BlockSpec((chunks, piece, chunk_rows), lambda n: (0, n, 0)),
        ],
        out_specs=pl.BlockSpec((width, piece), lambda n: (0, n)),
        out_shape=jax.ShapeDtypeStruct((width, hidden), jnp.float32),
        cost_estimate=estimate(2 * rows * width * hidden, 4 * width * hidden),
        name="first_gradient",
    )(inputs_t, slots)


def second_kernel(hidden_ref, incoming_ref, out_ref):
    chunks, rows, width = incoming_ref.shape
    active = jnp.maximum(hidden_ref[...], 0)
    out_ref[...] = dot(active, incoming_ref[...].reshape(chunks * rows, width), 1, 0)


def second_gradient(hidden_t, slots, chunks):
    hidden, rows = hidden_t.shape
    _, chunk_rows, width = slots.shape
    piece = piece_of(hidden, 640)
    return pl.pallas_call(
        second_kernel,
        grid=(hidden // piece,),
        in_specs=[
            pl.BlockSpec((piece, rows), lambda n: (n, 0)),
            pl.BlockSpec((chunks, chunk_rows, width), lambda n: (0, 0, 0)),
        ],
        out_specs=pl.BlockSpec((piece, width), lambda n: (n, 0)),
        out_shape=jax.ShapeDtypeStruct((hidden, width), jnp.float32),
        cost_estimate=estimate(2 * rows * width * hidden, 4 * width * hidden),
        name="second_gradient",
    )(hidden_t, slots)


def rows_last(parts):
    return parts.transpose(4, 0, 2, 1, 3).reshape(parts.shape[-1], -1)


def per_device(w_first, w_second, saved_inputs, saved_hidden, cotangent):
    sections = lax.axis_size("section")
    hids = lax.axis_size("hid")
    wids = lax.axis_size("wid")
    section = lax.axis_index("section")
    wid = lax.axis_index("wid")
    hid = lax.axis_index("hid")
    behind = LAG * (sections - 1 - section)
    is_last = (section == sections - 1).astype(jnp.int32)
    weight_first = w_first[0]
    weight_second = w_second[0]
    micro, rows, width = cotangent.shape
    hidden = saved_hidden.shape[-1]
    sub = rows // hids // SUB_CHUNKS
    chunk_rows = hids * sub
    chunks = micro * SUB_CHUNKS
    periods = chunks + LAG * (sections - 1)
    parts = (micro, hids, SUB_CHUNKS, sub)
    cot_parts = cotangent.reshape(*parts, width)
    hidden_t = rows_last(saved_hidden.reshape(*parts, hidden))
    inputs_t = rows_last(saved_inputs.reshape(*parts, width))
    wid_order = lax.rem(wid + 1 + jnp.arange(wids, dtype=jnp.int32), wids)
    hid_order = lax.rem(hid + 1 + jnp.arange(hids, dtype=jnp.int32), hids)
    hid_senders = lax.rem(hid + hids - jnp.arange(hids, dtype=jnp.int32), hids)

    incoming_slots = jnp.zeros((periods, chunk_rows, width), jnp.bfloat16)
    grad_slots = jnp.zeros((periods, hidden, chunk_rows), jnp.bfloat16)
    result_slots = jnp.zeros((periods, sub, width), jnp.bfloat16)
    nothing = [jnp.zeros((sub, width), jnp.bfloat16)] * hids
    received = {}
    for period in range(periods):
        slot = jnp.maximum(period - behind, 0)
        chosen = jnp.minimum(slot, chunks - 1)
        m, j = chosen // SUB_CHUNKS, lax.rem(chosen, SUB_CHUNKS)
        taken = is_last if period in received else jnp.int32(1)
        place = jnp.concatenate([jnp.stack([taken, m, j]), hid_senders, wid_order])
        sent, own, incoming = project(
            place, cot_parts, received.get(period, nothing), weight_second, wids
        )
        arrived = exchange(sent, "wid")
        block_grad = join(jnp.stack([wid, chosen]), own, arrived, hidden_t)
        hidden_grad = lax.all_gather(block_grad, "wid", axis=0, tiled=True)
        incoming_slots = lax.dynamic_update_slice_in_dim(incoming_slots, incoming[None], slot, 0)
        grad_slots = lax.dynamic_update_slice_in_dim(grad_slots, hidden_grad[None], slot, 0)
        shares = back(hid_order, hidden_grad, weight_first, hids)
        arrived = exchange(shares[:-1], "hid")
        row_share = rounded_total(shares[-1], arrived)
        result_slots = lax.dynamic_update_slice_in_dim(result_slots, row_share[None], slot, 0)
        if period + LAG < periods:
            received[period + LAG] = hand_down(row_share)

    grad_second = second_gradient(hidden_t, incoming_slots, chunks)
    grad_first = first_gradient(inputs_t, grad_slots, chunks)
    input_grads = result_slots[:chunks].reshape(micro, SUB_CHUNKS * sub, width)
    return (grad_first[None], grad_second[None], input_grads[None])


def solution(mesh):
    placed = (
        P("section", "wid", "hid"),
        P("section", "hid", "wid"),
        P("section", None, None, "wid"),
        P("section", None, None, "hid"),
        P(None, None, "wid"),
    )

    def step(*arrays):
        return jax.shard_map(
            per_device,
            mesh=mesh,
            in_specs=placed,
            out_specs=(
                P("section", "wid", "hid"),
                P("section", "hid", "wid"),
                P("section", None, "hid", "wid"),
            ),
            check_vma=False,
        )(*arrays)

    return step
```

```python
import functools

import jax
import jax.numpy as jnp
from jax import lax
from jax.experimental import pallas as pl
from jax.experimental.pallas import tpu as pltpu
from jax.sharding import PartitionSpec as P

SUB_CHUNKS = 2
LAG = 2
PROJECT_PIECE = 640
REST_PIECE = 1280
BACK_PIECE = 640
HID_SENT_AS = jnp.float32


def exchange(blocks, axis):
    count = lax.axis_size(axis)
    arrived = []
    for shift in range(1, count):
        pairs = [(i, (i + shift) % count) for i in range(count)]
        arrived.append(lax.ppermute(blocks[shift - 1], axis, pairs))
    return arrived


def swap(block, axis, bit):
    pairs = [(i, i ^ bit) for i in range(lax.axis_size(axis))]
    return lax.ppermute(block, axis, pairs)


def bits_of(count):
    assert count & (count - 1) == 0, count
    return [1 << k for k in range(count.bit_length() - 1)]


def mask_order(count):
    odd = sorted(range(1, count, 2), reverse=True)
    return odd + sorted(range(0, count, 2), reverse=True)


def reduce_blocks(blocks, axis):
    count = lax.axis_size(axis)
    held = dict(blocks)
    mine = []
    for bit in bits_of(count):
        arrived = {}
        for m in mask_order(count):
            if m in held and m & bit:
                arrived[m ^ bit] = swap(held.pop(m), axis, bit)
        mine.append(arrived.pop(0))
        for m, block in arrived.items():
            if isinstance(held[m], list):
                held[m] = held[m] + [block]
            else:
                held[m] = [held[m], block]
        for m in list(held):
            if m and m & (2 * bit) and isinstance(held[m], list):
                held[m] = rounded_total(held[m][0], held[m][1:])
    return held[0], mine


def gather_blocks(block, axis):
    held = {0: block}
    for bit in reversed(bits_of(lax.axis_size(axis))):
        held.update({m ^ bit: swap(b, axis, bit) for m, b in held.items()})
    return held


def hand_down(share):
    sections, hids = lax.axis_size("section"), lax.axis_size("hid")
    arrived = []
    for shift in range(hids):
        pairs = [
            (s * hids + h, (s - 1) * hids + (h + shift) % hids)
            for s in range(1, sections)
            for h in range(hids)
        ]
        arrived.append(lax.ppermute(share, ("section", "hid"), pairs))
    return arrived


def estimate(flops, moved):
    return pl.CostEstimate(flops=flops, bytes_accessed=moved, transcendentals=0)


def dot(left, right, left_dim, right_dim):
    return lax.dot_general(
        left, right, (((left_dim,), (right_dim,)), ((), ())), preferred_element_type=jnp.float32
    )


def piece_of(size, wanted):
    fits = [p for p in range(128, wanted + 1, 128) if size % p == 0]
    return fits[-1] if fits else size


class Places:
    def __init__(self, wids, hids):
        self.section, self.wid, self.ordered = 0, 1, 2
        self.by_mask = self.ordered + wids
        self.senders = self.by_mask + wids
        self.row_blocks = self.senders + hids
        self.periods = self.row_blocks + hids

    def period(self, number):
        return self.periods + 4 * number


def project_kernel(hids, given_at, senders_at, table_ref, given_ref, *refs):
    received_refs, weight_ref, (block_ref, turned_ref, incoming_ref) = (
        refs[:hids],
        refs[hids],
        refs[hids + 1 :],
    )
    rows, width = incoming_ref.shape
    sub = rows // hids

    @pl.when(pl.program_id(0) == 0)
    def _():
        @pl.when(table_ref[given_at] == 1)
        def _():
            incoming_ref[...] = given_ref[...].reshape(rows, width)

        @pl.when(table_ref[given_at] != 1)
        def _():
            for k in range(hids):
                start = pl.multiple_of(table_ref[senders_at + k] * sub, sub)
                incoming_ref[pl.ds(start, sub), :] = received_refs[k][...]

        turned_ref[...] = incoming_ref[...].T

    block_ref[...] = dot(weight_ref[...], turned_ref[...], 1, 0).astype(block_ref.dtype)


def project(table, places, period, given_parts, received, weight, count):
    hidden, width = weight.shape
    hids, _, sub = given_parts.shape[1:4]
    rows = hids * sub
    columns = hidden // count
    piece = piece_of(columns, PROJECT_PIECE)
    pieces = columns // piece
    at = places.period(period)
    grid_spec = pltpu.PrefetchScalarGridSpec(
        num_scalar_prefetch=1,
        grid=(pieces,),
        in_specs=[
            pl.BlockSpec((1, hids, 1, sub, width), lambda c, s: (s[at + 1], 0, s[at + 2], 0, 0)),
            *[pl.BlockSpec((sub, width), lambda c, s: (0, 0)) for _ in range(hids)],
            pl.BlockSpec((piece, width), lambda c, s: (s[places.ordered] * pieces + c, 0)),
        ],
        out_specs=[
            pl.BlockSpec((piece, rows), lambda c, s: (c, 0)),
            pl.BlockSpec((width, rows), lambda c, s: (0, 0)),
            pl.BlockSpec((rows, width), lambda c, s: (0, 0)),
        ],
    )
    return pl.pallas_call(
        functools.partial(project_kernel, hids, at, places.senders),
        grid_spec=grid_spec,
        out_shape=[
            jax.ShapeDtypeStruct((columns, rows), jnp.bfloat16),
            jax.ShapeDtypeStruct((width, rows), jnp.bfloat16),
            jax.ShapeDtypeStruct((rows, width), jnp.bfloat16),
        ],
        cost_estimate=estimate(2 * rows * width * columns, 2 * width * columns),
        name="project",
    )(table, given_parts, *received, weight)


def rest_kernel(table_ref, turned_ref, weight_ref, *out_refs):
    step = pl.program_id(0)
    block = dot(weight_ref[...], turned_ref[...], 1, 0)
    for k, ref in enumerate(out_refs):

        @pl.when(step == k)
        def _(ref=ref):
            ref[...] = block.astype(ref.dtype)


def rest(table, places, turned, weight, count):
    hidden, width = weight.shape
    rows = turned.shape[1]
    columns = hidden // count
    piece = piece_of(columns, REST_PIECE)
    pieces = columns // piece
    masks = mask_order(count)[1:]

    def block_at(own_step):
        def index(k, c, s):
            return (jnp.where(k == own_step, c, jnp.where(k < own_step, 0, pieces - 1)), 0)

        return pl.BlockSpec((piece, rows), index)

    grid_spec = pltpu.PrefetchScalarGridSpec(
        num_scalar_prefetch=1,
        grid=(count - 1, pieces),
        in_specs=[
            pl.BlockSpec((width, rows), lambda k, c, s: (0, 0)),
            pl.BlockSpec((piece, width), lambda k, c, s: (s[places.ordered + 1 + k] * pieces + c, 0)),
        ],
        out_specs=[block_at(k) for k in range(count - 1)],
    )
    out = pl.pallas_call(
        rest_kernel,
        grid_spec=grid_spec,
        out_shape=[
            jax.ShapeDtypeStruct((columns, rows), jnp.bfloat16 if m % 2 else jnp.float32)
            for m in masks
        ],
        cost_estimate=estimate(2 * rows * width * (hidden - columns), 2 * width * (hidden - columns)),
        name="rest",
    )(table, turned, weight)
    return dict(zip(masks, out))


def join_kernel(table_ref, own_ref, *refs):
    arrived_refs, (hidden_ref, out_ref) = refs[:-2], refs[-2:]
    total = own_ref[...]
    for ref in arrived_refs:
        total += ref[...].astype(jnp.float32)
    out_ref[...] = jnp.where(hidden_ref[...] > 0, total, jnp.float32(0.0)).astype(out_ref.dtype)


def join(table, places, period, own, arrived, hidden_t):
    columns, rows = own.shape
    piece = piece_of(columns, 640)
    pieces = columns // piece
    chunk_at = places.period(period) + 3
    here = pl.BlockSpec((piece, rows), lambda n, s: (n, 0))
    grid_spec = pltpu.PrefetchScalarGridSpec(
        num_scalar_prefetch=1,
        grid=(pieces,),
        in_specs=[here]
        + [here for _ in arrived]
        + [pl.BlockSpec((piece, rows), lambda n, s: (s[places.wid] * pieces + n, s[chunk_at]))],
        out_specs=here,
    )
    return pl.pallas_call(
        join_kernel,
        grid_spec=grid_spec,
        out_shape=jax.ShapeDtypeStruct(own.shape, jnp.bfloat16),
        cost_estimate=estimate(5 * own.size, 14 * own.size),
        name="join",
    )(table, own, *arrived, hidden_t)


def rounded_total(own, arrived):
    total = own
    for block in arrived:
        total = total + block.astype(jnp.float32)
    return total.astype(jnp.bfloat16)


def back_kernel(count, hids, places, table_ref, *refs):
    block_refs, weight_ref, refs = refs[:count], refs[count], refs[count + 1 :]
    out_refs, (grads_ref, piece_ref) = refs[:hids], refs[hids:]
    sub = out_refs[0].shape[0]
    columns = block_refs[0].shape[0]

    @pl.when(pl.program_id(0) == 0)
    def _():
        for m in range(count):
            start = pl.multiple_of(table_ref[places.by_mask + m] * columns, columns)
            grads_ref[pl.ds(start, columns), :] = block_refs[m][...]

    piece_ref[...] = dot(weight_ref[...], grads_ref[...], 1, 0).T
    for k in range(hids):
        start = pl.multiple_of(table_ref[places.row_blocks + k] * sub, sub)
        out_refs[k][...] = piece_ref[pl.ds(start, sub), :].astype(out_refs[k].dtype)


def back(table, places, blocks, weight, hids):
    columns, rows = blocks[0].shape
    count = len(blocks)
    width, hidden = weight.shape
    sub = rows // hids
    piece = piece_of(width, BACK_PIECE)
    grid_spec = pltpu.PrefetchScalarGridSpec(
        num_scalar_prefetch=1,
        grid=(width // piece,),
        in_specs=[
            *[pl.BlockSpec((columns, rows), lambda n, s: (0, 0)) for _ in range(count)],
            pl.BlockSpec((piece, hidden), lambda n, s: (n, 0)),
        ],
        out_specs=[
            *[pl.BlockSpec((sub, piece), lambda n, s: (0, n)) for _ in range(hids)],
            pl.BlockSpec((hidden, rows), lambda n, s: (0, 0)),
        ],
        scratch_shapes=[pltpu.VMEM((rows, piece), jnp.float32)],
    )
    out = pl.pallas_call(
        functools.partial(back_kernel, count, hids, places),
        grid_spec=grid_spec,
        out_shape=[
            *[jax.ShapeDtypeStruct((sub, width), HID_SENT_AS) for _ in range(hids - 1)],
            jax.ShapeDtypeStruct((sub, width), jnp.float32),
            jax.ShapeDtypeStruct((hidden, rows), jnp.bfloat16),
        ],
        cost_estimate=estimate(2 * rows * width * hidden, 2 * width * hidden),
        name="back",
    )(table, *[blocks[m] for m in range(count)], weight)
    return out[:hids], out[hids]


def pick(place_ref, candidates, write):
    for c, by_section in enumerate(candidates):
        for s, ref in enumerate(by_section):

            @pl.when(place_ref[0] == s)
            def _(c=c, ref=ref):
                write(c, ref)


def grouped(refs, sections):
    return [refs[i : i + sections] for i in range(0, len(refs), sections)]


def first_kernel(sections, place_ref, inputs_ref, *refs):
    candidates, (out_ref, grads_ref) = grouped(refs[:-2], sections), refs[-2:]

    def write(c, ref):
        rows = ref.shape[1]
        grads_ref[:, c * rows : (c + 1) * rows] = ref[...]

    pick(place_ref, candidates, write)
    out_ref[...] = dot(inputs_ref[...], grads_ref[...], 1, 1)


def first_gradient(place, inputs_t, candidates):
    width, rows = inputs_t.shape
    sections = len(candidates[0])
    hidden, chunk_rows = candidates[0][0].shape
    piece = piece_of(hidden, 640)

    def only_on(section):
        return pl.BlockSpec((piece, chunk_rows), lambda n, s: (jnp.where(s[0] == section, n, 0), 0))

    grid_spec = pltpu.PrefetchScalarGridSpec(
        num_scalar_prefetch=1,
        grid=(hidden // piece,),
        in_specs=[pl.BlockSpec((width, rows), lambda n, s: (0, 0))]
        + [only_on(s) for _ in candidates for s in range(sections)],
        out_specs=pl.BlockSpec((width, piece), lambda n, s: (0, n)),
        scratch_shapes=[pltpu.VMEM((piece, rows), jnp.bfloat16)],
    )
    return pl.pallas_call(
        functools.partial(first_kernel, sections),
        grid_spec=grid_spec,
        out_shape=jax.ShapeDtypeStruct((width, hidden), jnp.float32),
        cost_estimate=estimate(2 * rows * width * hidden, 4 * width * hidden),
        name="first_gradient",
    )(place, inputs_t, *[a for by_section in candidates for a in by_section])


def second_kernel(sections, place_ref, hidden_ref, *refs):
    candidates, (out_ref, incoming_ref) = grouped(refs[:-2], sections), refs[-2:]

    def write(c, ref):
        rows = ref.shape[0]
        incoming_ref[c * rows : (c + 1) * rows, :] = ref[...]

    @pl.when(pl.program_id(0) == 0)
    def _():
        pick(place_ref, candidates, write)

    active = jnp.maximum(hidden_ref[...], 0)
    out_ref[...] = dot(active, incoming_ref[...], 1, 0)


def second_gradient(place, hidden_t, candidates):
    hidden, rows = hidden_t.shape
    sections = len(candidates[0])
    chunk_rows, width = candidates[0][0].shape
    piece = piece_of(hidden, 640)
    whole = pl.BlockSpec((chunk_rows, width), lambda n, s: (0, 0))
    grid_spec = pltpu.PrefetchScalarGridSpec(
        num_scalar_prefetch=1,
        grid=(hidden // piece,),
        in_specs=[pl.BlockSpec((piece, rows), lambda n, s: (n, 0))]
        + [whole for _ in candidates for _ in range(sections)],
        out_specs=pl.BlockSpec((piece, width), lambda n, s: (n, 0)),
        scratch_shapes=[pltpu.VMEM((rows, width), jnp.bfloat16)],
    )
    return pl.pallas_call(
        functools.partial(second_kernel, sections),
        grid_spec=grid_spec,
        out_shape=jax.ShapeDtypeStruct((hidden, width), jnp.float32),
        cost_estimate=estimate(2 * rows * width * hidden, 4 * width * hidden),
        name="second_gradient",
    )(place, hidden_t, *[a for by_section in candidates for a in by_section])


def rows_last(parts):
    return parts.transpose(4, 0, 2, 1, 3).reshape(parts.shape[-1], -1)


def per_device(w_first, w_second, saved_inputs, saved_hidden, cotangent):
    sections = lax.axis_size("section")
    hids = lax.axis_size("hid")
    wids = lax.axis_size("wid")
    section = lax.axis_index("section")
    wid = lax.axis_index("wid")
    hid = lax.axis_index("hid")
    behind = LAG * (sections - 1 - section)
    is_last = (section == sections - 1).astype(jnp.int32)
    weight_first = w_first[0]
    weight_second = w_second[0]
    micro, rows, width = cotangent.shape
    hidden = saved_hidden.shape[-1]
    sub = rows // hids // SUB_CHUNKS
    chunks = micro * SUB_CHUNKS
    periods = chunks + LAG * (sections - 1)
    parts = (micro, hids, SUB_CHUNKS, sub)
    cot_parts = cotangent.reshape(*parts, width)
    hidden_t = rows_last(saved_hidden.reshape(*parts, hidden))
    inputs_t = rows_last(saved_inputs.reshape(*parts, width))
    places = Places(wids, hids)
    steps = jnp.arange(hids, dtype=jnp.int32)
    number = jnp.arange(periods, dtype=jnp.int32)
    chosen = jnp.clip(number - behind, 0, chunks - 1)
    given_now = jnp.where(number < LAG, 1, is_last)
    table = jnp.concatenate(
        [
            jnp.stack([section, wid]),
            wid ^ jnp.array(mask_order(wids), jnp.int32),
            wid ^ jnp.arange(wids, dtype=jnp.int32),
            lax.rem(hid + hids - steps, hids),
            lax.rem(hid + 1 + steps, hids),
            jnp.stack(
                [given_now, lax.div(chosen, SUB_CHUNKS), lax.rem(chosen, SUB_CHUNKS), chosen], axis=1
            ).reshape(-1),
        ]
    )

    nothing = [jnp.zeros((sub, width), jnp.bfloat16)] * hids
    received = {}
    incoming, grads, results = [], [], []
    for period in range(periods):
        first, turned, given = project(
            table, places, period, cot_parts, received.get(period, nothing), weight_second, wids
        )
        blocks = rest(table, places, turned, weight_second, wids)
        blocks[mask_order(wids)[0]] = first
        incoming.append(given)
        own, arrived = reduce_blocks(blocks, "wid")
        block_grad = join(table, places, period, own, arrived, hidden_t)
        gathered = gather_blocks(block_grad, "wid")
        shares, hidden_grad = back(table, places, gathered, weight_first, hids)
        grads.append(hidden_grad)
        arrived = exchange(shares[:-1], "hid")
        row_share = rounded_total(shares[-1], arrived)
        results.append(lax.optimization_barrier(row_share))
        if period + LAG < periods:
            received[period + LAG] = hand_down(row_share)

    def by_chunk(values):
        return [
            [values[c + LAG * (sections - 1 - s)] for s in range(sections)] for c in range(chunks)
        ]

    grad_second = second_gradient(table, hidden_t, by_chunk(incoming))
    grad_first = first_gradient(table, inputs_t, by_chunk(grads))
    input_grads = jnp.stack(
        [lax.select_n(section, *by_section) if sections > 1 else by_section[0]
         for by_section in by_chunk(results)]
    ).reshape(micro, SUB_CHUNKS * sub, width)
    return (grad_first[None], grad_second[None], input_grads[None])


def solution(mesh):
    placed = (
        P("section", "wid", "hid"),
        P("section", "hid", "wid"),
        P("section", None, None, "wid"),
        P("section", None, None, "hid"),
        P(None, None, "wid"),
    )

    def step(*arrays):
        return jax.shard_map(
            per_device,
            mesh=mesh,
            in_specs=placed,
            out_specs=(
                P("section", "wid", "hid"),
                P("section", "hid", "wid"),
                P("section", None, "hid", "wid"),
            ),
            check_vma=False,
        )(*arrays)

    return step
```

```python
import functools

import jax
import jax.numpy as jnp
from jax import lax
from jax.experimental import pallas as pl
from jax.experimental.pallas import tpu as pltpu
from jax.sharding import PartitionSpec as P

SUB_CHUNKS = 2
LAG = 2
PROJECT_PIECE = 640
REST_PIECE = 1280
BACK_PIECE = 640
HID_SENT_AS = jnp.float32
LANES = 128


def exchange(blocks, axis):
    count = lax.axis_size(axis)
    arrived = []
    for shift in range(1, count):
        pairs = [(i, (i + shift) % count) for i in range(count)]
        arrived.append(lax.ppermute(blocks[shift - 1], axis, pairs))
    return arrived


def swap(block, axis, bit):
    pairs = [(i, i ^ bit) for i in range(lax.axis_size(axis))]
    return lax.ppermute(block, axis, pairs)


def bits_of(count):
    assert count & (count - 1) == 0, count
    return [1 << k for k in range(count.bit_length() - 1)]


def mask_order(count):
    odd = sorted(range(1, count, 2), reverse=True)
    return odd + sorted(range(0, count, 2), reverse=True)


def reduce_blocks(blocks, axis):
    count = lax.axis_size(axis)
    held = dict(blocks)
    mine = []
    for bit in bits_of(count):
        arrived = {}
        for m in mask_order(count):
            if m in held and m & bit:
                arrived[m ^ bit] = swap(held.pop(m), axis, bit)
        mine.append(arrived.pop(0))
        for m, block in arrived.items():
            if isinstance(held[m], list):
                held[m] = held[m] + [block]
            else:
                held[m] = [held[m], block]
        for m in list(held):
            if m and m & (2 * bit) and isinstance(held[m], list):
                held[m] = rounded_total(held[m][0], held[m][1:])
    return held[0], mine


def gather_blocks(block, axis):
    held = {0: block}
    for bit in reversed(bits_of(lax.axis_size(axis))):
        held.update({m ^ bit: swap(b, axis, bit) for m, b in held.items()})
    return held


def hand_down(share):
    sections, hids = lax.axis_size("section"), lax.axis_size("hid")
    arrived = []
    for shift in range(hids):
        pairs = [
            (s * hids + h, (s - 1) * hids + (h + shift) % hids)
            for s in range(1, sections)
            for h in range(hids)
        ]
        arrived.append(lax.ppermute(share, ("section", "hid"), pairs))
    return arrived


def estimate(flops, moved):
    return pl.CostEstimate(flops=flops, bytes_accessed=moved, transcendentals=0)


def dot(left, right, left_dim, right_dim):
    return lax.dot_general(
        left, right, (((left_dim,), (right_dim,)), ((), ())), preferred_element_type=jnp.float32
    )


def piece_of(size, wanted):
    fits = [p for p in range(128, wanted + 1, 128) if size % p == 0]
    return fits[-1] if fits else size


class Places:
    def __init__(self, wids, hids):
        self.section, self.wid, self.ordered = 0, 1, 2
        self.by_mask = self.ordered + wids
        self.senders = self.by_mask + wids
        self.row_blocks = self.senders + hids
        self.periods = self.row_blocks + hids

    def period(self, number):
        return self.periods + 4 * number


def project_kernel(hids, given_at, senders_at, table_ref, given_ref, *refs):
    received_refs, weight_ref, (block_ref, turned_ref, incoming_ref) = (
        refs[:hids],
        refs[hids],
        refs[hids + 1 :],
    )
    rows, width = incoming_ref.shape
    sub = rows // hids

    @pl.when(pl.program_id(0) == 0)
    def _():
        @pl.when(table_ref[given_at] == 1)
        def _():
            incoming_ref[...] = given_ref[...].reshape(rows, width)

        @pl.when(table_ref[given_at] != 1)
        def _():
            for k in range(hids):
                start = pl.multiple_of(table_ref[senders_at + k] * sub, sub)
                incoming_ref[pl.ds(start, sub), :] = received_refs[k][...]

        turned_ref[...] = incoming_ref[...].T

    block_ref[...] = dot(weight_ref[...], turned_ref[...], 1, 0).astype(block_ref.dtype)


def project(table, places, period, given_parts, received, weight, count):
    hidden, width = weight.shape
    hids, _, sub = given_parts.shape[1:4]
    rows = hids * sub
    columns = hidden // count
    piece = piece_of(columns, PROJECT_PIECE)
    pieces = columns // piece
    at = places.period(period)
    grid_spec = pltpu.PrefetchScalarGridSpec(
        num_scalar_prefetch=1,
        grid=(pieces,),
        in_specs=[
            pl.BlockSpec((1, hids, 1, sub, width), lambda c, s: (s[at + 1], 0, s[at + 2], 0, 0)),
            *[pl.BlockSpec((sub, width), lambda c, s: (0, 0)) for _ in range(hids)],
            pl.BlockSpec((piece, width), lambda c, s: (s[places.ordered] * pieces + c, 0)),
        ],
        out_specs=[
            pl.BlockSpec((piece, rows), lambda c, s: (c, 0)),
            pl.BlockSpec((width, rows), lambda c, s: (0, 0)),
            pl.BlockSpec((rows, width), lambda c, s: (0, 0)),
        ],
    )
    return pl.pallas_call(
        functools.partial(project_kernel, hids, at, places.senders),
        grid_spec=grid_spec,
        out_shape=[
            jax.ShapeDtypeStruct((columns, rows), jnp.bfloat16),
            jax.ShapeDtypeStruct((width, rows), jnp.bfloat16),
            jax.ShapeDtypeStruct((rows, width), jnp.bfloat16),
        ],
        cost_estimate=estimate(2 * rows * width * columns, 2 * width * columns),
        name="project",
    )(table, given_parts, *received, weight)


def rest_kernel(table_ref, turned_ref, weight_ref, *out_refs):
    step = pl.program_id(0)
    block = dot(weight_ref[...], turned_ref[...], 1, 0)
    for k, ref in enumerate(out_refs):

        @pl.when(step == k)
        def _(ref=ref):
            ref[...] = block.astype(ref.dtype)


def rest(table, places, turned, weight, count):
    hidden, width = weight.shape
    rows = turned.shape[1]
    columns = hidden // count
    piece = piece_of(columns, REST_PIECE)
    pieces = columns // piece
    masks = mask_order(count)[1:]

    def block_at(own_step):
        def index(k, c, s):
            return (jnp.where(k == own_step, c, jnp.where(k < own_step, 0, pieces - 1)), 0)

        return pl.BlockSpec((piece, rows), index)

    grid_spec = pltpu.PrefetchScalarGridSpec(
        num_scalar_prefetch=1,
        grid=(count - 1, pieces),
        in_specs=[
            pl.BlockSpec((width, rows), lambda k, c, s: (0, 0)),
            pl.BlockSpec((piece, width), lambda k, c, s: (s[places.ordered + 1 + k] * pieces + c, 0)),
        ],
        out_specs=[block_at(k) for k in range(count - 1)],
    )
    out = pl.pallas_call(
        rest_kernel,
        grid_spec=grid_spec,
        out_shape=[
            jax.ShapeDtypeStruct((columns, rows), jnp.bfloat16 if m % 2 else jnp.float32)
            for m in masks
        ],
        cost_estimate=estimate(2 * rows * width * (hidden - columns), 2 * width * (hidden - columns)),
        name="rest",
    )(table, turned, weight)
    return dict(zip(masks, out))


def join_kernel(table_ref, own_ref, *refs):
    arrived_refs, (hidden_ref, out_ref) = refs[:-2], refs[-2:]
    total = own_ref[...]
    for ref in arrived_refs:
        total += ref[...].astype(jnp.float32)
    out_ref[...] = jnp.where(hidden_ref[...] > 0, total, jnp.float32(0.0)).astype(out_ref.dtype)


def join(table, places, period, own, arrived, hidden_t):
    columns, rows = own.shape
    piece = piece_of(columns, 640)
    pieces = columns // piece
    chunk_at = places.period(period) + 3
    here = pl.BlockSpec((piece, rows), lambda n, s: (n, 0))
    grid_spec = pltpu.PrefetchScalarGridSpec(
        num_scalar_prefetch=1,
        grid=(pieces,),
        in_specs=[here]
        + [here for _ in arrived]
        + [pl.BlockSpec((piece, rows), lambda n, s: (s[places.wid] * pieces + n, s[chunk_at]))],
        out_specs=here,
    )
    return pl.pallas_call(
        join_kernel,
        grid_spec=grid_spec,
        out_shape=jax.ShapeDtypeStruct(own.shape, jnp.bfloat16),
        cost_estimate=estimate(5 * own.size, 14 * own.size),
        name="join",
    )(table, own, *arrived, hidden_t)


def rounded_total(own, arrived):
    total = own
    for block in arrived:
        total = total + block.astype(jnp.float32)
    return total.astype(jnp.bfloat16)


def back_kernel(count, hids, places, table_ref, *refs):
    block_refs, weight_ref, refs = refs[:count], refs[count], refs[count + 1 :]
    out_refs, (grads_ref, piece_ref) = refs[:hids], refs[hids:]
    sub = out_refs[0].shape[0]
    columns = block_refs[0].shape[0]

    @pl.when(pl.program_id(0) == 0)
    def _():
        for m in range(count):
            start = pl.multiple_of(table_ref[places.by_mask + m] * columns, columns)
            grads_ref[pl.ds(start, columns), :] = block_refs[m][...]

    piece_ref[...] = dot(weight_ref[...], grads_ref[...], 1, 0).T
    for k in range(hids):
        start = pl.multiple_of(table_ref[places.row_blocks + k] * sub, sub)
        out_refs[k][...] = piece_ref[pl.ds(start, sub), :].astype(out_refs[k].dtype)


def back(table, places, blocks, weight, hids):
    columns, rows = blocks[0].shape
    count = len(blocks)
    width, hidden = weight.shape
    sub = rows // hids
    piece = piece_of(width, BACK_PIECE)
    grid_spec = pltpu.PrefetchScalarGridSpec(
        num_scalar_prefetch=1,
        grid=(width // piece,),
        in_specs=[
            *[pl.BlockSpec((columns, rows), lambda n, s: (0, 0)) for _ in range(count)],
            pl.BlockSpec((piece, hidden), lambda n, s: (n, 0)),
        ],
        out_specs=[
            *[pl.BlockSpec((sub, piece), lambda n, s: (0, n)) for _ in range(hids)],
            pl.BlockSpec((hidden, rows), lambda n, s: (0, 0)),
        ],
        scratch_shapes=[pltpu.VMEM((rows, piece), jnp.float32)],
    )
    out = pl.pallas_call(
        functools.partial(back_kernel, count, hids, places),
        grid_spec=grid_spec,
        out_shape=[
            *[jax.ShapeDtypeStruct((sub, width), HID_SENT_AS) for _ in range(hids - 1)],
            jax.ShapeDtypeStruct((sub, width), jnp.float32),
            jax.ShapeDtypeStruct((hidden, rows), jnp.bfloat16),
        ],
        cost_estimate=estimate(2 * rows * width * hidden, 2 * width * hidden),
        name="back",
    )(table, *[blocks[m] for m in range(count)], weight)
    return out[:hids], out[hids]


def pick(place_ref, candidates, write):
    for c, by_section in enumerate(candidates):
        for s, ref in enumerate(by_section):

            @pl.when(place_ref[0] == s)
            def _(c=c, ref=ref):
                write(c, ref)


def grouped(refs, sections):
    return [refs[i : i + sections] for i in range(0, len(refs), sections)]


def first_kernel(sections, masks, table_ref, inputs_ref, *refs):
    out_ref, grads_ref = refs[-2:]
    late = refs[: len(masks)]
    candidates = grouped(refs[len(masks) : -2], sections)
    rows = late[0].shape[1]

    for c, by_section in enumerate(candidates):
        for s, ref in enumerate(by_section):
            if (c, s) == (len(candidates) - 1, 0):
                for k, last_ref in enumerate(late):

                    @pl.when((table_ref[0] == s) & (pl.program_id(0) == k))
                    def _(c=c, last_ref=last_ref):
                        grads_ref[:, c * rows : (c + 1) * rows] = last_ref[...]

            else:

                @pl.when(table_ref[0] == s)
                def _(c=c, ref=ref):
                    grads_ref[:, c * rows : (c + 1) * rows] = ref[...]

    out_ref[...] = dot(inputs_ref[...], grads_ref[...], 1, 1)


def more_first_kernel(sections, masks, table_ref, so_far_ref, *refs):
    first_kernel(sections, masks, table_ref, *refs)


def first_gradient(table, places, masks, inputs_t, last, candidates, so_far=None):
    width, rows = inputs_t.shape
    sections = len(candidates[0])
    hidden, chunk_rows = candidates[0][0].shape
    columns = last[0].shape[0]
    piece = piece_of(columns, 640)
    if piece % 128:
        piece = columns
    pieces = columns // piece

    def block_of(k, s):
        block = s[places.by_mask + masks[0]]
        for i, m in enumerate(masks[1:], 1):
            block = jnp.where(k == i, s[places.by_mask + m], block)
        return block

    def only_on(section, unused):
        def index(k, c, s):
            here = block_of(k, s) * pieces + c
            return (0 if unused else jnp.where(s[0] == section, here, 0), 0)

        return pl.BlockSpec((piece, chunk_rows), index)

    def late_at(own_step):
        return pl.BlockSpec((piece, chunk_rows), lambda k, c, s: (jnp.where(k == own_step, c, 0), 0))

    earlier = [] if so_far is None else [so_far]
    kernel = first_kernel if so_far is None else more_first_kernel
    grid_spec = pltpu.PrefetchScalarGridSpec(
        num_scalar_prefetch=1,
        grid=(len(masks), pieces),
        in_specs=[pl.BlockSpec(memory_space=pl.ANY) for _ in earlier]
        + [pl.BlockSpec((width, rows), lambda k, c, s: (0, 0))]
        + [late_at(k) for k in range(len(masks))]
        + [
            only_on(s, (c, s) == (len(candidates) - 1, 0))
            for c in range(len(candidates))
            for s in range(sections)
        ],
        out_specs=pl.BlockSpec((width, piece), lambda k, c, s: (0, block_of(k, s) * pieces + c)),
        scratch_shapes=[pltpu.VMEM((piece, rows), jnp.bfloat16)],
    )
    share = len(masks) * columns
    return pl.pallas_call(
        functools.partial(kernel, sections, masks),
        grid_spec=grid_spec,
        out_shape=jax.ShapeDtypeStruct((width, hidden), jnp.float32),
        input_output_aliases={} if so_far is None else {1: 0},
        cost_estimate=estimate(2 * rows * width * share, 4 * width * share),
        name="first_gradient",
    )(
        table,
        *earlier,
        inputs_t,
        *[last[m] for m in masks],
        *[a for by_section in candidates for a in by_section],
    )


def whole_first_gradient(inputs_t, section, candidates):
    grads = jnp.concatenate([lax.select_n(section, *by_section) for by_section in candidates], axis=1)
    return dot(inputs_t, grads, 1, 1)


def second_kernel(sections, place_ref, hidden_ref, *refs):
    candidates, (out_ref, incoming_ref) = grouped(refs[:-2], sections), refs[-2:]

    def write(c, ref):
        rows = ref.shape[0]
        incoming_ref[c * rows : (c + 1) * rows, :] = ref[...]

    @pl.when(pl.program_id(0) == 0)
    def _():
        pick(place_ref, candidates, write)

    active = jnp.maximum(hidden_ref[...], 0)
    out_ref[...] = dot(active, incoming_ref[...], 1, 0)


def second_gradient(place, hidden_t, candidates):
    hidden, rows = hidden_t.shape
    sections = len(candidates[0])
    chunk_rows, width = candidates[0][0].shape
    piece = piece_of(hidden, 640)
    whole = pl.BlockSpec((chunk_rows, width), lambda n, s: (0, 0))
    grid_spec = pltpu.PrefetchScalarGridSpec(
        num_scalar_prefetch=1,
        grid=(hidden // piece,),
        in_specs=[pl.BlockSpec((piece, rows), lambda n, s: (n, 0))]
        + [whole for _ in candidates for _ in range(sections)],
        out_specs=pl.BlockSpec((piece, width), lambda n, s: (n, 0)),
        scratch_shapes=[pltpu.VMEM((rows, width), jnp.bfloat16)],
    )
    return pl.pallas_call(
        functools.partial(second_kernel, sections),
        grid_spec=grid_spec,
        out_shape=jax.ShapeDtypeStruct((hidden, width), jnp.float32),
        cost_estimate=estimate(2 * rows * width * hidden, 4 * width * hidden),
        name="second_gradient",
    )(place, hidden_t, *[a for by_section in candidates for a in by_section])


def rows_last(parts):
    return parts.transpose(4, 0, 2, 1, 3).reshape(parts.shape[-1], -1)


def per_device(w_first, w_second, saved_inputs, saved_hidden, cotangent):
    sections = lax.axis_size("section")
    hids = lax.axis_size("hid")
    wids = lax.axis_size("wid")
    section = lax.axis_index("section")
    wid = lax.axis_index("wid")
    hid = lax.axis_index("hid")
    behind = LAG * (sections - 1 - section)
    is_last = (section == sections - 1).astype(jnp.int32)
    weight_first = w_first[0]
    weight_second = w_second[0]
    micro, rows, width = cotangent.shape
    hidden = saved_hidden.shape[-1]
    columns = hidden // wids
    sub = rows // hids // SUB_CHUNKS
    chunks = micro * SUB_CHUNKS
    periods = chunks + LAG * (sections - 1)
    parts = (micro, hids, SUB_CHUNKS, sub)
    cot_parts = cotangent.reshape(*parts, width)
    hidden_t = rows_last(saved_hidden.reshape(*parts, hidden))
    inputs_t = rows_last(saved_inputs.reshape(*parts, width))
    places = Places(wids, hids)
    steps = jnp.arange(hids, dtype=jnp.int32)
    number = jnp.arange(periods, dtype=jnp.int32)
    chosen = jnp.clip(number - behind, 0, chunks - 1)
    given_now = jnp.where(number < LAG, 1, is_last)
    table = jnp.concatenate(
        [
            jnp.stack([section, wid]),
            wid ^ jnp.array(mask_order(wids), jnp.int32),
            wid ^ jnp.arange(wids, dtype=jnp.int32),
            lax.rem(hid + hids - steps, hids),
            lax.rem(hid + 1 + steps, hids),
            jnp.stack(
                [given_now, lax.div(chosen, SUB_CHUNKS), lax.rem(chosen, SUB_CHUNKS), chosen], axis=1
            ).reshape(-1),
        ]
    )

    nothing = [jnp.zeros((sub, width), jnp.bfloat16)] * hids
    received = {}
    incoming, grads, results = [], [], []
    for period in range(periods):
        first, turned, given = project(
            table, places, period, cot_parts, received.get(period, nothing), weight_second, wids
        )
        blocks = rest(table, places, turned, weight_second, wids)
        blocks[mask_order(wids)[0]] = first
        incoming.append(given)
        own, arrived = reduce_blocks(blocks, "wid")
        block_grad = join(table, places, period, own, arrived, hidden_t)
        gathered = gather_blocks(block_grad, "wid")
        shares, hidden_grad = back(table, places, gathered, weight_first, hids)
        grads.append(hidden_grad)
        arrived = exchange(shares[:-1], "hid")
        row_share = rounded_total(shares[-1], arrived)
        results.append(lax.optimization_barrier(row_share))
        if period + LAG < periods:
            received[period + LAG] = hand_down(row_share)

    def by_chunk(values):
        return [
            [values[c + LAG * (sections - 1 - s)] for s in range(sections)] for c in range(chunks)
        ]

    grad_second = second_gradient(table, hidden_t, by_chunk(incoming))
    if columns % LANES:
        grad_first = whole_first_gradient(inputs_t, section, by_chunk(grads))
    else:
        earlier = by_chunk(grads)
        earlier[-1][0] = grads[0]
        early = first_gradient(
            table, places, list(range(0, wids, 2)), inputs_t, gathered, earlier
        )
        grad_first = first_gradient(
            table, places, list(range(1, wids, 2)), inputs_t, gathered, earlier, early
        )
    input_grads = jnp.stack(
        [lax.select_n(section, *by_section) if sections > 1 else by_section[0]
         for by_section in by_chunk(results)]
    ).reshape(micro, SUB_CHUNKS * sub, width)
    return (grad_first[None], grad_second[None], input_grads[None])


def solution(mesh):
    placed = (
        P("section", "wid", "hid"),
        P("section", "hid", "wid"),
        P("section", None, None, "wid"),
        P("section", None, None, "hid"),
        P(None, None, "wid"),
    )

    def step(*arrays):
        return jax.shard_map(
            per_device,
            mesh=mesh,
            in_specs=placed,
            out_specs=(
                P("section", "wid", "hid"),
                P("section", "hid", "wid"),
                P("section", None, "hid", "wid"),
            ),
            check_vma=False,
        )(*arrays)

    return step
```
